32 devices in a mesh: shift: 2 (over y), space: 4 (over z), orb: 2 (over x), grid: 2 (over core).
Axes of the slice: x: 2, y: 2, z: 4, core: 2. Of those that a mesh axis runs over, the one named last changes fastest.
Arguments:
- support: bfloat16 [128, 9, 15, 256], P(('shift', 'space', 'orb'), None, None, 'grid'), parts along dimension 0, may hold values from -0.75 to 0.75
- anchor: int32 [128], P(('shift', 'space', 'orb')), parts along dimension 0, may hold values from 0 to 63, as said below
- kernel: float32 [512, 9, 9], P(('shift', 'space', 'orb')), parts along dimension 0, may hold values from -2.1 to 2.1
- pair_owner: int32 [512], P(('shift', 'space', 'orb')), parts along dimension 0, may hold values from 0 to 63, as said below
- pair_partner: int32 [512], P(('shift', 'space', 'orb')), parts along dimension 0, may hold values from 0 to 63, as said below
- pair_live: int32 [512], P(('shift', 'space', 'orb')), parts along dimension 0, may hold values 0 or 1
- v_ext: float32 [128, 256], P(('shift', 'space'), 'grid'), parts along dimension 0, may hold values from -6 to 6
Outputs:
- density: float32 [128, 256], P(('shift', 'space'), 'grid'), parts along dimension 0
- hamiltonian: float32 [512, 9, 9], P(('shift', 'space', 'orb')), parts along dimension 0
The draws below stay inside these ranges and needn't reach their ends.
There are 2 independent parts, one for each index of `shift`. The reference program is written for one: setup_inputs(seed, part) draws one part's arguments, and reference() takes and returns one part's arrays. A program takes and returns all parts, laid end to end along the dimension named above; each array names one. Nothing has to cross between parts.
Inputs may be any that keep to these rules, and one draw needn't show every extreme that they name: Atom a lies in spatial domain a // 16, and its box starts at a plane of that domain: anchor[a] // 16 = a // 16. The owner of slot p is one of the 8 atoms of block p // 32: pair_owner[p] // 8 = p // 32. `pair_partner`: the partner of a slot lies in its owner's spatial domain or in one of the two adjacent domains, counted periodically, and its box shares at least one plane with the owner's box: |gap| <= 14.
All inputs are finite; a program needn't handle non-finite values. No bound on the sum of `pair_live` on one device may be relied on, other than what follows from the above.
Results may differ from the reference program's by a relative error of at most 0.0028.
Values may be sent and summed in bfloat16 or wider, within the bound.
A program may use at most 64 MiB of HBM per device.

```python
import jax
import jax.numpy as jnp
from jax import lax

NSF = 9
BZ = 15
PLANE = 256
SLAB = 16
ATOM_DEV = 8
PAIR_DEV = 32
ATOM_DOM = 16
ATOMS = 64
PAIRS = 256
NZ = 64


def anchor_table(key):
    rows = jnp.arange(ATOMS, dtype=jnp.int32)
    home = rows // ATOM_DOM
    offset = jax.random.randint(jax.random.fold_in(key, 11), (ATOMS,), 0, SLAB, dtype=jnp.int32)
    return (home * SLAB + offset).astype(jnp.int32)


def owner_table(key):
    slots = jnp.arange(PAIRS, dtype=jnp.int32)
    block = slots // PAIR_DEV
    pick = jax.random.randint(jax.random.fold_in(key, 23), (PAIRS,), 0, ATOM_DEV, dtype=jnp.int32)
    return (block * ATOM_DEV + pick).astype(jnp.int32)


def draw_anchor(key, part):
    return anchor_table(key)


def draw_pair_owner(key, part):
    return owner_table(key)


def draw_pair_partner(key, part):
    starts = anchor_table(key)
    owners = owner_table(key)
    domains = ATOMS // ATOM_DOM
    home = owners // ATOM_DOM
    width = 3 * ATOM_DOM
    column = jnp.arange(width, dtype=jnp.int32)[None, :]
    cand_domain = (home[:, None] - 1 + column // ATOM_DOM + domains) % domains
    candidate = (cand_domain * ATOM_DOM + column % ATOM_DOM).astype(jnp.int32)
    gap = (starts[owners][:, None] - starts[candidate] + NZ // 2) % NZ - NZ // 2
    fits = jnp.abs(gap) <= BZ - 1
    noise = jax.random.randint(jax.random.fold_in(key, 37), (PAIRS, width), 0, 1048576, dtype=jnp.int32)
    score = jnp.where(fits, noise * width + column, -1)
    best = jnp.argmax(score, axis=1).astype(jnp.int32)
    return jnp.take_along_axis(candidate, best[:, None], axis=1)[:, 0].astype(jnp.int32)


def touch_ends(result, key, low, high):
    shape = result.shape
    place = [jax.random.randint(jax.random.fold_in(key, axis), (), 0, shape[axis]) for axis in range(len(shape))]
    result = result.at[tuple(place)].set(low)
    longest = shape.index(max(shape))
    place[longest] = (place[longest] + 1) % shape[longest]
    return result.at[tuple(place)].set(high)


def steps_of(key, shape, pieces, low, high):
    gain = 1.0
    for position, shards_of in pieces:
        steps = jax.random.uniform(jax.random.fold_in(jax.random.fold_in(key, 6), position), (shards_of,), jnp.float32, low / len(pieces), high / len(pieces))
        gain = gain * jnp.repeat(jnp.exp(steps), shape[position] // shards_of).reshape((-1,) + (1,) * (len(shape) - 1 - position))
    return gain


def scatter_about(stream_key, shape, scale, limit, split=(), kind=jnp.bfloat16):
    level = steps_of(stream_key, shape, split, -0.22, 0.18) if split else 1.0
    result = jax.random.normal(stream_key, shape, jnp.float32) * scale * level
    return jnp.minimum(jnp.maximum(result, -limit), limit).astype(kind)


def setup_inputs(seed: int = 0, part: int = 0) -> dict:
    keys = jax.random.split(jax.random.key(seed), 8)
    part_splits = jax.random.split(jax.random.fold_in(keys[7], part), 8)
    return {
        "support": scatter_about(part_splits[0], (ATOMS, NSF, BZ, PLANE), 0.125, 0.75, ((0, 8), (3, 2))),
        "anchor": draw_anchor(jax.random.fold_in(jax.random.fold_in(keys[7], part), 71), part),
        "kernel": scatter_about(part_splits[2], (PAIRS, NSF, NSF), 0.35, 2.1, ((0, 8),), jnp.float32),
        "pair_owner": draw_pair_owner(jax.random.fold_in(jax.random.fold_in(keys[7], part), 71), part),
        "pair_partner": draw_pair_partner(jax.random.fold_in(jax.random.fold_in(keys[7], part), 71), part),
        "pair_live": touch_ends((jax.random.randint(part_splits[5], (PAIRS,), 0, 4) < 3).astype(jnp.int32), jax.random.fold_in(part_splits[5], 1), 0, 1),
        "v_ext": scatter_about(part_splits[6], (NZ, PLANE), 1.0, 6.0, ((0, 4), (1, 2)), jnp.float32),
    }


def shift_planes(rows, plane_gap, box_depth):
    index = jnp.arange(box_depth, dtype=jnp.int32)[None, :] + plane_gap[:, None]
    inside = (index >= 0) & (index < box_depth)
    picked = jnp.take_along_axis(rows, jnp.clip(index, 0, box_depth - 1)[:, None, :, None], axis=2)
    return jnp.where(inside[:, None, :, None], picked, jnp.zeros_like(picked))

def reference(support, anchor, kernel, pair_owner, pair_partner, pair_live, v_ext):
    blocks = PAIRS // PAIR_DEV
    owners = pair_owner.reshape(blocks, PAIR_DEV)
    partners = pair_partner.reshape(blocks, PAIR_DEV)
    live = pair_live.astype(jnp.float32).reshape(blocks, PAIR_DEV)
    weights = kernel.reshape(blocks, PAIR_DEV, NSF, NSF)
    block_ids = jnp.arange(blocks, dtype=jnp.int32)

    def moved_rows(own, part):
        plane_gap = (anchor[own] - anchor[part] + NZ // 2) % NZ - NZ // 2
        return shift_planes(support[part], plane_gap.astype(jnp.int32), BZ)

    def block_aux(items):
        own, part, alive, kern, block = items
        moved = moved_rows(own, part).astype(jnp.float32)
        terms = jnp.einsum('pst,ptjq->psjq', kern * alive[:, None, None], moved, precision=lax.Precision.HIGHEST)
        local = (own - block * ATOM_DEV).astype(jnp.int32)
        return jax.ops.segment_sum(terms, local, num_segments=ATOM_DEV)
    aux = lax.map(block_aux, (owners, partners, live, weights, block_ids))
    aux = aux.reshape(ATOMS, NSF, BZ, PLANE)
    deposit = lax.optimization_barrier(jnp.sum(support.astype(jnp.float32) * aux, axis=1))
    planes = (anchor[:, None] + jnp.arange(BZ, dtype=jnp.int32)[None, :]) % NZ
    density = jnp.zeros((NZ, PLANE), jnp.float32).at[planes.reshape(-1)].add(deposit.reshape(-1, PLANE))
    potential = v_ext + density / jnp.sqrt(1.0 + density * density)
    box_potential = potential[planes]
    weighted = (support.astype(jnp.float32) * box_potential[:, None, :, :]).astype(jnp.bfloat16)

    def block_ham(items):
        own, part, alive = items
        moved = moved_rows(own, part).astype(jnp.float32)
        rows = weighted[own].astype(jnp.float32)
        blocks_out = jnp.einsum('psjq,ptjq->pst', rows, moved, precision=lax.Precision.HIGHEST)
        return blocks_out * alive[:, None, None]
    hamiltonian = lax.map(block_ham, (owners, partners, live)).reshape(PAIRS, NSF, NSF)
    return (density, hamiltonian)
```

```python
import functools

import jax
import jax.numpy as jnp
from jax import lax
from jax.experimental import pallas as pl
from jax.experimental.pallas import tpu as pltpu
from jax.sharding import PartitionSpec as P

LANES = 128
MESH = pl.DeviceIdType.MESH
F32 = jnp.float32
BF16 = jnp.bfloat16


def dot(a, b):
    return lax.dot_general(a, b, (((1,), (0,)), ((), ())), preferred_element_type=F32)


def dot_t(a, b):
    return lax.dot_general(a, b, (((1,), (1,)), ((), ())), preferred_element_type=F32)


def split(value):
    high = value.astype(BF16)
    return high, (value - high.astype(F32)).astype(BF16)


def respond(field):
    return field / jnp.sqrt(1.0 + field * field)


class Plan:
    def __init__(self, support, kernel, v_ext, orbs, spaces):
        self.atoms, self.funcs, self.depth, self.points = support.shape
        self.pairs = kernel.shape[0]
        self.slab = v_ext.shape[0]
        self.orbs, self.spaces = orbs, spaces
        self.blocks = 2 * orbs
        self.rows = self.slab // orbs
        self.width = self.rows * self.points
        self.block = (self.funcs + self.funcs % 2) * self.atoms
        self.total = self.blocks * self.block
        over = self.depth - 1
        self.even = over % orbs == 0 and (self.slab - over) % orbs == 0
        self.zrows = over // orbs if self.even else self.rows
        self.square = self.funcs * self.funcs
        self.over = over
        cut = (self.zrows + 1) // 2
        self.chunks = [(0, cut), (cut, self.zrows)]
        if self.zrows < self.rows:
            self.chunks.append((self.zrows, self.rows))

    def plane(self, orb, i):
        if not self.even:
            return orb * self.rows + i
        if i < self.zrows:
            return orb * self.zrows + i
        return self.over + orb * (self.rows - self.zrows) + i - self.zrows


def body(
    pn,
    meta_ref,
    support_ref,
    v_ref,
    density_ref,
    ham_ref,
    pad,
    packed,
    boxes,
    metas,
    masked,
    kmat,
    aux,
    gmat,
    weighted,
    dens,
    hpart,
    hrecv,
    xs_sem,
    xr_sem,
    zs_sem,
    zr_sem,
    ms_sem,
    mr_sem,
    ds_sem,
    dr_sem,
    hs_sem,
    hr_sem,
):
    n, space_count = pn.orbs, pn.spaces
    A, F, Q = pn.atoms, pn.funcs, pn.points
    orb, dom, grid = lax.axis_index("orb"), lax.axis_index("space"), lax.axis_index("grid")
    above, below = lax.rem(dom + 1, space_count), lax.rem(dom + space_count - 1, space_count)

    def peer(k):
        return lax.rem(orb + k, n)

    barrier = pltpu.get_barrier_semaphore()
    met = 0
    for place in (dom, above, below):
        for k in range(n):
            for g in range(2):
                if place is dom and k == 0 and g == 0:
                    continue
                pl.semaphore_signal(
                    barrier,
                    inc=1,
                    device_id={"space": place, "orb": peer(k), "grid": lax.rem(grid + g, 2)},
                    device_id_type=MESH,
                )
                met += 1

    pad[...] = jnp.zeros_like(pad)
    pad[:, :, 0 : pn.depth, :] = support_ref[...]
    step = pad.shape[2]
    lane = lax.broadcasted_iota(jnp.int32, (A, A * step), 1)
    sub = lax.broadcasted_iota(jnp.int32, (A, A * step), 0)
    j = lane - sub * step
    mine = (j >= 0) & (j < pn.depth)
    offset = jnp.broadcast_to(meta_ref[0:A, pn.square + 3 : pn.square + 4], (A, A * step))
    spot = offset.astype(jnp.int32) + j
    place_rows = []
    for o in range(n):
        for i in range(pn.rows):
            r = pn.plane(o, i)
            hit = mine & ((spot == r) | (spot == r + pn.slab))
            place_rows.append(jnp.where(hit, 1.0, 0.0))
    placing = jnp.concatenate(place_rows, axis=0).astype(BF16)
    aligned = []
    for s in range(F):
        aligned.append(dot(placing, pad[:, s].reshape(A * step, Q)))
    nothing = jnp.zeros((A, Q), F32)
    for o in range(n):
        for i in range(pn.rows):
            base = (o * pn.rows + i) * A
            for s in range(0, F, 2):
                first = aligned[s][base : base + A]
                second = aligned[s + 1][base : base + A] if s + 1 < F else nothing
                packed[o, s * A : (s + 2) * A, i * Q : (i + 1) * Q] = jnp.concatenate(
                    [first, second], axis=0
                ).astype(BF16)

    pl.semaphore_wait(barrier, met)

    sends = []

    def send(src, dst, ssem, rsem, where):
        copy = pltpu.make_async_remote_copy(
            src_ref=src, dst_ref=dst, send_sem=ssem, recv_sem=rsem,
            device_id=where, device_id_type=MESH,
        )
        copy.start()
        sends.append(copy)

    def arrive(dst, ssem, rsem):
        pltpu.make_async_remote_copy(
            src_ref=dst, dst_ref=dst, send_sem=ssem, recv_sem=rsem,
            device_id={"space": above}, device_id_type=MESH,
        ).wait_recv()

    for k in range(1, n):
        send(meta_ref, metas.at[n + orb], ms_sem.at[k], mr_sem.at[n + orb], {"orb": peer(k)})
    for k in range(n):
        send(
            meta_ref, metas.at[orb], ms_sem.at[n + k], mr_sem.at[orb],
            {"space": above, "orb": peer(k)},
        )
    for c, (lo, hi) in enumerate(pn.chunks):
        cols = pl.ds(lo * Q, (hi - lo) * Q)
        for k in range(1, n):
            send(
                packed.at[peer(k), :, cols], boxes.at[n + orb, :, cols],
                xs_sem.at[k, c], xr_sem.at[orb, c], {"orb": peer(k)},
            )
        if c < 2:
            send(
                packed.at[orb, :, cols], boxes.at[orb, :, cols],
                zs_sem.at[0, c], zr_sem.at[orb, c], {"space": above},
            )
    boxes[n + orb] = packed[orb]
    metas[n + orb] = meta_ref[...]
    for c, (lo, hi) in enumerate(pn.chunks):
        cols = pl.ds(lo * Q, (hi - lo) * Q)
        for k in range(1, n):
            other = peer(k)
            arrive(boxes.at[n + other, :, cols], xs_sem.at[k, c], xr_sem.at[other, c])
            if c < 2:
                send(
                    boxes.at[n + other, :, cols], boxes.at[other, :, cols],
                    zs_sem.at[k, c], zr_sem.at[other, c], {"space": above},
                )
    for k in range(1, n):
        other = peer(k)
        arrive(metas.at[n + other], ms_sem.at[k], mr_sem.at[n + other])
    for o in range(n):
        arrive(metas.at[o], ms_sem.at[n], mr_sem.at[o])

    everyone = pn.blocks * pn.pairs
    table = metas[...].reshape(everyone, LANES)
    holder = lax.broadcasted_iota(jnp.int32, (everyone, 1), 0) // pn.pairs
    partner = table[:, pn.square : pn.square + 1].astype(jnp.int32)
    partner = partner - jnp.where(holder < n, n * A, 0)
    owner = table[:, pn.square + 1 : pn.square + 2].astype(jnp.int32) + holder * A

    def columns(shape, axis):
        col = lax.broadcasted_iota(jnp.int32, shape, axis)
        blk = jnp.zeros(shape, jnp.int32)
        for b in range(1, pn.blocks):
            blk = blk + jnp.where(col >= b * pn.block, 1, 0)
        rest = col - blk * pn.block
        func = rest // A
        return blk * A + (rest - func * A), func

    code, func = columns((everyone, pn.total), 1)
    picks = jnp.where((code == partner) & (func < F), 1.0, 0.0)
    picks16 = picks.astype(BF16)
    owner_lane = lax.broadcasted_iota(jnp.int32, (everyone, LANES), 1)
    owns = jnp.where(owner_lane == owner, 1.0, 0.0)
    owns_t = owns.T[0 : pn.blocks * A].astype(BF16)
    owns16 = owns[:, 0 : pn.blocks * A].astype(BF16)
    table_hi, table_lo = split(table)
    spread_row = lax.broadcasted_iota(jnp.int32, (LANES, pn.total), 0)
    _, spread_func = columns((LANES, pn.total), 1)
    spread_func = jnp.where(spread_func < F, spread_func, -pn.square)
    kmat[...] = jnp.zeros_like(kmat)
    for s in range(F):
        spread = jnp.where(spread_row == s * F + spread_func, 1.0, 0.0).astype(BF16)
        q_hi = dot(table_hi, spread).astype(BF16) * picks16
        q_lo = dot(table_lo, spread).astype(BF16) * picks16
        rows = dot(owns_t, q_hi) + dot(owns_t, q_lo)
        for b in range(pn.blocks):
            kmat[b * pn.block + s * A : b * pn.block + (s + 1) * A, :] = rows[b * A : (b + 1) * A]
    k_hi, k_lo = split(kmat[...])

    for k in range(n):
        other = peer(k)
        for c, (lo, hi) in enumerate(pn.chunks[:2]):
            cols = pl.ds(lo * Q, (hi - lo) * Q)
            arrive(boxes.at[other, :, cols], zs_sem.at[k, c], zr_sem.at[other, c])

    for b in range(pn.blocks):
        start = jnp.broadcast_to(metas[b, 0:A, pn.square + 3 : pn.square + 4], (A, Q))
        start = jnp.concatenate([start] * 2, axis=0).astype(jnp.int32)
        for i in range(pn.rows):
            cols = slice(i * Q, (i + 1) * Q)
            if b < n and i >= pn.zrows:
                masked[b * pn.block : (b + 1) * pn.block, cols] = jnp.zeros((pn.block, Q), BF16)
                continue
            r = pn.plane(orb, i)
            keep = (start <= r) if b >= n else (start > r)
            for t in range(pn.block // (2 * A)):
                part = boxes[b, t * 2 * A : (t + 1) * 2 * A, cols].astype(F32)
                masked[b * pn.block + t * 2 * A : b * pn.block + (t + 1) * 2 * A, cols] = jnp.where(
                    keep, part, 0.0
                ).astype(BF16)

    aux[...] = dot(k_hi, masked[...]) + dot(k_lo, masked[...])
    for i in range(pn.rows):
        cols = slice(i * Q, (i + 1) * Q)
        x = masked[:, cols].astype(F32)
        line = jnp.sum(x * aux[:, cols], axis=0, keepdims=True)
        dens[orb, pl.ds(i, 1), :] = line
        potential = v_ref[pl.ds(pn.plane(orb, i), 1), :] + respond(line)
        weighted[:, cols] = (x * potential).astype(BF16)
    for k in range(1, n):
        send(dens.at[orb], dens.at[orb], ds_sem.at[k], dr_sem.at[orb], {"orb": peer(k)})
    gmat[...] = dot_t(weighted[...], masked[...])

    gather_col = lax.broadcasted_iota(jnp.int32, (pn.total, LANES), 1)
    _, gather_func = columns((pn.total, LANES), 0)
    gather_func = jnp.where(gather_func < F, gather_func, -pn.square)
    found = jnp.zeros((everyone, LANES), F32)
    for s in range(F):
        rows = jnp.concatenate(
            [gmat[b * pn.block + s * A : b * pn.block + (s + 1) * A, :] for b in range(pn.blocks)],
            axis=0,
        )
        r_hi, r_lo = split(rows)
        t_hi, t_lo = split((dot(owns16, r_hi) + dot(owns16, r_lo)) * picks)
        gather = jnp.where(gather_col == s * F + gather_func, 1.0, 0.0).astype(BF16)
        found = found + dot(t_hi, gather) + dot(t_lo, gather)
    hpart[...] = found.reshape(pn.blocks, pn.pairs, LANES)

    count = 0
    for up in (1, 0):
        for k in range(n):
            for g in range(2):
                if up == 0 and k == 0 and g == 0:
                    continue
                blk = peer(k) if up else n + peer(k)
                slot = (up * n + orb) * 2 + grid
                send(
                    hpart.at[blk], hrecv.at[slot], hs_sem.at[count], hr_sem.at[slot],
                    {
                        "space": below if up else dom,
                        "orb": peer(k),
                        "grid": lax.rem(grid + g, 2),
                    },
                )
                count += 1
    hrecv[orb * 2 + grid] = hpart[n + orb]
    for k in range(1, n):
        other = peer(k)
        arrive(dens.at[other], ds_sem.at[k], dr_sem.at[other])
    for o in range(n):
        for i in range(pn.rows):
            r = pn.plane(o, i)
            density_ref[r : r + 1, :] = dens[o, i : i + 1, :]
    for up in (0, 1):
        for k in range(n):
            for g in range(2):
                if up == 0 and k == 0 and g == 0:
                    continue
                slot = (up * n + peer(k)) * 2 + lax.rem(grid + g, 2)
                arrive(hrecv.at[slot], hs_sem.at[0], hr_sem.at[slot])
    total = hrecv[0]
    for slot in range(1, 2 * pn.blocks):
        total = total + hrecv[slot]
    ham_ref[...] = total * meta_ref[:, pn.square + 2 : pn.square + 3]
    for copy in sends:
        copy.wait_send()


def on_device(support, anchor, kernel, pair_owner, pair_partner, pair_live, v_ext):
    orb_count, space_count = lax.axis_size("orb"), lax.axis_size("space")
    pn = Plan(support, kernel, v_ext, orb_count, space_count)
    domain, orb_index = lax.axis_index("space"), lax.axis_index("orb")
    per_domain = pn.atoms * orb_count
    own_block = domain * orb_count + orb_index
    partner_domain = pair_partner // per_domain
    relative = (partner_domain - domain + 1 + space_count) % space_count
    code = relative * per_domain + pair_partner % per_domain
    owner = pair_owner - own_block * pn.atoms
    alive = pair_live.astype(F32)
    offset = jnp.pad((anchor - domain * pn.slab).astype(F32), (0, pn.pairs - pn.atoms))
    meta = jnp.concatenate(
        [
            (kernel * alive[:, None, None]).reshape(pn.pairs, pn.square),
            jnp.stack([code.astype(F32), owner.astype(F32), alive, offset], axis=1),
            jnp.zeros((pn.pairs, LANES - pn.square - 4), F32),
        ],
        axis=1,
    )
    n, C = pn.orbs, len(pn.chunks)
    vmem = pl.BlockSpec(memory_space=pltpu.VMEM)
    dma = pltpu.SemaphoreType.DMA
    step = -(-pn.depth // 16) * 16
    density, packed = pl.pallas_call(
        functools.partial(body, pn),
        out_shape=(
            jax.ShapeDtypeStruct(v_ext.shape, F32),
            jax.ShapeDtypeStruct((pn.pairs, LANES), F32),
        ),
        in_specs=[vmem] * 3,
        out_specs=(vmem, vmem),
        scratch_shapes=[
            pltpu.VMEM((pn.atoms, pn.funcs, step, pn.points), BF16),
            pltpu.VMEM((n, pn.block, pn.width), BF16),
            pltpu.VMEM((pn.blocks, pn.block, pn.width), BF16),
            pltpu.VMEM((pn.blocks, pn.pairs, LANES), F32),
            pltpu.VMEM((pn.total, pn.width), BF16),
            pltpu.VMEM((pn.total, pn.total), F32),
            pltpu.VMEM((pn.total, pn.width), F32),
            pltpu.VMEM((pn.total, pn.total), F32),
            pltpu.VMEM((pn.total, pn.width), BF16),
            pltpu.VMEM((n, pn.rows, pn.points), F32),
            pltpu.VMEM((pn.blocks, pn.pairs, LANES), F32),
            pltpu.VMEM((2 * pn.blocks, pn.pairs, LANES), F32),
            dma((n, C)),
            dma((n, C)),
            dma((n, 2)),
            dma((n, 2)),
            dma((2 * n,)),
            dma((2 * n,)),
            dma((n,)),
            dma((n,)),
            dma((2 * pn.blocks,)),
            dma((2 * pn.blocks,)),
        ],
        compiler_params=pltpu.CompilerParams(collective_id=0, has_side_effects=True),
        name="grain",
    )(meta, support, v_ext)
    hamiltonian = packed[:, : pn.square].reshape(pn.pairs, pn.funcs, pn.funcs)
    return (density, hamiltonian)


def solution(mesh):
    placed = (
        P(("shift", "space", "orb"), None, None, "grid"),
        P(("shift", "space", "orb")),
        P(("shift", "space", "orb"), None, None),
        P(("shift", "space", "orb")),
        P(("shift", "space", "orb")),
        P(("shift", "space", "orb")),
        P(("shift", "space"), "grid"),
    )
    return jax.shard_map(
        on_device,
        mesh=mesh,
        in_specs=placed,
        out_specs=(P(("shift", "space"), "grid"), P(("shift", "space", "orb"), None, None)),
        check_vma=False,
    )
```

```python
import functools

import jax
import jax.numpy as jnp
from jax import lax
from jax.experimental import pallas as pl
from jax.experimental.pallas import tpu as pltpu
from jax.sharding import PartitionSpec as P

LANES = 128
MESH = pl.DeviceIdType.MESH
F32 = jnp.float32
BF16 = jnp.bfloat16


def dot(a, b):
    return lax.dot_general(a, b, (((1,), (0,)), ((), ())), preferred_element_type=F32)


def dot_t(a, b):
    return lax.dot_general(a, b, (((1,), (1,)), ((), ())), preferred_element_type=F32)


def respond(field):
    return field / jnp.sqrt(1.0 + field * field)


class Plan:
    def __init__(self, support, kernel, v_ext, orbs, spaces):
        self.atoms, self.funcs, self.depth, self.points = support.shape
        self.pairs = kernel.shape[0]
        self.slab = v_ext.shape[0]
        self.orbs, self.spaces = orbs, spaces
        self.blocks = 2 * orbs
        self.rows = self.slab // orbs
        self.width = self.rows * self.points
        self.block = (self.funcs + self.funcs % 2) * self.atoms
        self.total = self.blocks * self.block
        over = self.depth - 1
        self.even = over % orbs == 0 and (self.slab - over) % orbs == 0
        self.zrows = over // orbs if self.even else self.rows
        self.square = self.funcs * self.funcs
        self.over = over
        cut = (self.zrows + 1) // 2
        self.chunks = [(0, cut), (cut, self.zrows)]
        if self.zrows < self.rows:
            self.chunks.append((self.zrows, self.rows))

    def plane(self, orb, i):
        if not self.even:
            return orb * self.rows + i
        if i < self.zrows:
            return orb * self.zrows + i
        return self.over + orb * (self.rows - self.zrows) + i - self.zrows


def body(
    pn,
    kernel_ref,
    owner_ref,
    partner_ref,
    live_ref,
    anchor_ref,
    support_ref,
    v_ref,
    density_ref,
    ham_ref,
    turned,
    meta_ref,
    chooser,
    packed,
    boxes,
    metas,
    masked,
    kmat,
    aux,
    gmat,
    weighted,
    dens,
    hpart,
    hrecv,
    xs_sem,
    xr_sem,
    zs_sem,
    zr_sem,
    ms_sem,
    mr_sem,
    ds_sem,
    dr_sem,
    hs_sem,
    hr_sem,
):
    n, space_count = pn.orbs, pn.spaces
    A, F, Q = pn.atoms, pn.funcs, pn.points
    orb, dom, grid = lax.axis_index("orb"), lax.axis_index("space"), lax.axis_index("grid")
    above, below = lax.rem(dom + 1, space_count), lax.rem(dom + space_count - 1, space_count)

    def peer(k):
        return lax.rem(orb + k, n)

    barrier = pltpu.get_barrier_semaphore()
    met = 0
    for place in (dom, above, below):
        for k in range(n):
            for g in range(2):
                if place is dom and k == 0 and g == 0:
                    continue
                pl.semaphore_signal(
                    barrier,
                    inc=1,
                    device_id={"space": place, "orb": peer(k), "grid": lax.rem(grid + g, 2)},
                    device_id_type=MESH,
                )
                met += 1

    domain_atoms = A * n
    alive = live_ref[...].astype(F32)
    turned[...] = jnp.zeros_like(turned)
    for s in range(F):
        turned[s * F : (s + 1) * F, 0 : pn.pairs] = kernel_ref[s] * alive
    away = partner_ref[...] // domain_atoms
    within = partner_ref[...] - away * domain_atoms
    away = away - dom + 1
    away = jnp.where(away < 0, away + space_count, away)
    away = jnp.where(away >= space_count, away - space_count, away)
    base = pn.square
    turned[base : base + 1, 0 : pn.pairs] = (away * domain_atoms + within).astype(F32)
    turned[base + 1 : base + 2, 0 : pn.pairs] = (owner_ref[...] - (dom * n + orb) * A).astype(F32)
    turned[base + 2 : base + 3, 0 : pn.pairs] = alive
    turned[base + 3 : base + 4, 0:A] = (anchor_ref[...] - dom * pn.slab).astype(F32)
    meta_ref[...] = turned[...].T[0 : pn.pairs]

    held = pn.depth * A
    lane = lax.broadcasted_iota(jnp.int32, (A, held), 1)
    sub = lax.broadcasted_iota(jnp.int32, (A, held), 0)
    j = lane // A
    mine = lane - j * A == sub
    offset = jnp.broadcast_to(meta_ref[0:A, pn.square + 3 : pn.square + 4], (A, held))
    spot = offset.astype(jnp.int32) + j
    place_rows = []
    for o in range(n):
        for i in range(pn.rows):
            r = pn.plane(o, i)
            hit = mine & ((spot == r) | (spot == r + pn.slab))
            place_rows.append(jnp.where(hit, 1.0, 0.0))
    placing = jnp.concatenate(place_rows, axis=0).astype(BF16)
    aligned = []
    for s in range(F):
        rows = support_ref[s].astype(F32).reshape(held, Q).astype(BF16)
        aligned.append(dot(placing, rows))
    nothing = jnp.zeros((A, Q), F32)
    for o in range(n):
        for i in range(pn.rows):
            base = (o * pn.rows + i) * A
            for s in range(0, F, 2):
                first = aligned[s][base : base + A]
                second = aligned[s + 1][base : base + A] if s + 1 < F else nothing
                packed[o, s * A : (s + 2) * A, i * Q : (i + 1) * Q] = jnp.concatenate(
                    [first, second], axis=0
                ).astype(BF16)

    pl.semaphore_wait(barrier, met)

    sends = []

    def send(src, dst, ssem, rsem, where):
        copy = pltpu.make_async_remote_copy(
            src_ref=src, dst_ref=dst, send_sem=ssem, recv_sem=rsem,
            device_id=where, device_id_type=MESH,
        )
        copy.start()
        sends.append(copy)

    def arrive(dst, ssem, rsem):
        pltpu.make_async_remote_copy(
            src_ref=dst, dst_ref=dst, send_sem=ssem, recv_sem=rsem,
            device_id={"space": above}, device_id_type=MESH,
        ).wait_recv()

    for k in range(1, n):
        send(meta_ref, metas.at[n + orb], ms_sem.at[k], mr_sem.at[n + orb], {"orb": peer(k)})
    for k in range(n):
        send(
            meta_ref, metas.at[orb], ms_sem.at[n + k], mr_sem.at[orb],
            {"space": above, "orb": peer(k)},
        )
    for c, (lo, hi) in enumerate(pn.chunks):
        cols = pl.ds(lo * Q, (hi - lo) * Q)
        for k in range(1, n):
            send(
                packed.at[peer(k), :, cols], boxes.at[n + orb, :, cols],
                xs_sem.at[k, c], xr_sem.at[orb, c], {"orb": peer(k)},
            )
        if c < 2:
            send(
                packed.at[orb, :, cols], boxes.at[orb, :, cols],
                zs_sem.at[0, c], zr_sem.at[orb, c], {"space": above},
            )
    everyone = pn.blocks * pn.pairs

    def columns(shape, axis):
        col = lax.broadcasted_iota(jnp.int32, shape, axis)
        blk = jnp.zeros(shape, jnp.int32)
        for b in range(1, pn.blocks):
            blk = blk + jnp.where(col >= b * pn.block, 1, 0)
        rest = col - blk * pn.block
        func = rest // A
        return blk * A + (rest - func * A), func

    code, func = columns((1, pn.total), 1)
    gather_col = lax.broadcasted_iota(jnp.int32, (pn.total, LANES), 1)
    _, gather_func = columns((pn.total, 1), 0)
    gather_func = jnp.where(gather_func < F, gather_func, -pn.square)
    gather_diff = gather_col - gather_func
    for s in range(F):
        chooser[s] = jnp.where(gather_diff == s * F, 1.0, 0.0).astype(BF16)
    boxes[n + orb] = packed[orb]
    metas[n + orb] = meta_ref[...]
    for c, (lo, hi) in enumerate(pn.chunks):
        cols = pl.ds(lo * Q, (hi - lo) * Q)
        for k in range(1, n):
            other = peer(k)
            arrive(boxes.at[n + other, :, cols], xs_sem.at[k, c], xr_sem.at[other, c])
            if c < 2:
                send(
                    boxes.at[n + other, :, cols], boxes.at[other, :, cols],
                    zs_sem.at[k, c], zr_sem.at[other, c], {"space": above},
                )
    for k in range(1, n):
        other = peer(k)
        arrive(metas.at[n + other], ms_sem.at[k], mr_sem.at[n + other])
    for o in range(n):
        arrive(metas.at[o], ms_sem.at[n], mr_sem.at[o])

    table = metas[...].reshape(everyone, LANES)
    holder = lax.broadcasted_iota(jnp.int32, (everyone, 1), 0) // pn.pairs
    partner = table[:, pn.square : pn.square + 1].astype(jnp.int32)
    partner = partner - jnp.where(holder < n, n * A, 0)
    owner = table[:, pn.square + 1 : pn.square + 2].astype(jnp.int32) + holder * A
    picks = jnp.where((code == partner) & (func < F), 1.0, 0.0)
    picks16 = picks.astype(BF16)
    owner_lane = lax.broadcasted_iota(jnp.int32, (everyone, LANES), 1)
    owns = jnp.where(owner_lane == owner, 1.0, 0.0)
    owns_t = owns.T[0 : pn.blocks * A].astype(BF16)
    owns16 = owns[:, 0 : pn.blocks * A].astype(BF16)
    table16 = table.astype(BF16)
    spread_row = lax.broadcasted_iota(jnp.int32, (LANES, pn.total), 0)
    spread_diff = spread_row - jnp.where(func < F, func, -pn.square)
    for b in range(pn.blocks):
        kmat[b * pn.block + F * A : (b + 1) * pn.block, :] = jnp.zeros(
            (pn.block - F * A, pn.total), F32
        )
    for s in range(F):
        spread = jnp.where(spread_diff == s * F, 1.0, 0.0).astype(BF16)
        rows = dot(owns_t, dot(table16, spread).astype(BF16) * picks16)
        for b in range(pn.blocks):
            kmat[b * pn.block + s * A : b * pn.block + (s + 1) * A, :] = rows[b * A : (b + 1) * A]
    k16 = kmat[...].astype(BF16)
    low = n * pn.block

    def keep_planes(b, lo, hi):
        start = jnp.broadcast_to(metas[b, 0:A, pn.square + 3 : pn.square + 4], (A, Q))
        start = jnp.concatenate([start] * 2, axis=0).astype(jnp.int32)
        for i in range(lo, hi):
            cols = slice(i * Q, (i + 1) * Q)
            r = pn.plane(orb, i)
            keep = (start <= r) if b >= n else (start > r)
            for t in range(pn.block // (2 * A)):
                part = boxes[b, t * 2 * A : (t + 1) * 2 * A, cols].astype(F32)
                masked[b * pn.block + t * 2 * A : b * pn.block + (t + 1) * 2 * A, cols] = jnp.where(
                    keep, part, 0.0
                ).astype(BF16)

    for b in range(n, pn.blocks):
        keep_planes(b, 0, pn.rows)
    aux[...] = dot(k16[:, low:], masked[low:, :])
    gmat[...] = jnp.zeros_like(gmat)
    for c in list(range(2, len(pn.chunks))) + [0, 1]:
        lo, hi = pn.chunks[c]
        span = slice(lo * Q, hi * Q)
        if c < 2:
            cols = pl.ds(lo * Q, (hi - lo) * Q)
            for k in range(n):
                other = peer(k)
                arrive(boxes.at[other, :, cols], zs_sem.at[k, c], zr_sem.at[other, c])
            for b in range(n):
                keep_planes(b, lo, hi)
            aux[:, span] = aux[:, span] + dot(k16[:, :low], masked[:low, span])
        else:
            masked[:low, span] = jnp.zeros((low, (hi - lo) * Q), BF16)
        for i in range(lo, hi):
            cols = slice(i * Q, (i + 1) * Q)
            x = masked[:, cols].astype(F32)
            line = jnp.sum(x * aux[:, cols], axis=0, keepdims=True)
            dens[orb, pl.ds(i, 1), :] = line
            potential = v_ref[pl.ds(pn.plane(orb, i), 1), :] + respond(line)
            weighted[:, cols] = (x * potential).astype(BF16)
        gmat[...] = gmat[...] + dot_t(weighted[:, span], masked[:, span])
    for k in range(1, n):
        send(dens.at[orb], dens.at[orb], ds_sem.at[k], dr_sem.at[orb], {"orb": peer(k)})

    found = jnp.zeros((everyone, LANES), F32)
    for s in range(F):
        rows = jnp.concatenate(
            [gmat[b * pn.block + s * A : b * pn.block + (s + 1) * A, :] for b in range(pn.blocks)],
            axis=0,
        ).astype(BF16)
        found = found + dot(dot(owns16, rows).astype(BF16) * picks16, chooser[s])
    hpart[...] = found.astype(BF16).reshape(pn.blocks, pn.pairs, LANES)

    count = 0
    for up in (1, 0):
        for k in range(n):
            for g in range(2):
                if up == 0 and k == 0 and g == 0:
                    continue
                blk = peer(k) if up else n + peer(k)
                slot = (up * n + orb) * 2 + grid
                send(
                    hpart.at[blk], hrecv.at[slot], hs_sem.at[count], hr_sem.at[slot],
                    {
                        "space": below if up else dom,
                        "orb": peer(k),
                        "grid": lax.rem(grid + g, 2),
                    },
                )
                count += 1
    hrecv[orb * 2 + grid] = hpart[n + orb]
    for k in range(1, n):
        other = peer(k)
        arrive(dens.at[other], ds_sem.at[k], dr_sem.at[other])
    for o in range(n):
        for i in range(pn.rows):
            r = pn.plane(o, i)
            density_ref[r : r + 1, :] = dens[o, i : i + 1, :]
    for up in (0, 1):
        for k in range(n):
            for g in range(2):
                if up == 0 and k == 0 and g == 0:
                    continue
                slot = (up * n + peer(k)) * 2 + lax.rem(grid + g, 2)
                arrive(hrecv.at[slot], hs_sem.at[0], hr_sem.at[slot])
    total = hrecv[0].astype(F32)
    for slot in range(1, 2 * pn.blocks):
        total = total + hrecv[slot].astype(F32)
    ham_ref[...] = total * meta_ref[:, pn.square + 2 : pn.square + 3]
    for copy in sends:
        copy.wait_send()


def finish(pn, plane_ref, block_ref, density_ref, ham_ref):
    density_ref[...] = plane_ref[...]
    rows = block_ref[...].T
    for s in range(pn.funcs):
        ham_ref[s] = rows[s * pn.funcs : (s + 1) * pn.funcs, :]


def on_device(support, anchor, kernel, pair_owner, pair_partner, pair_live, v_ext):
    orb_count, space_count = lax.axis_size("orb"), lax.axis_size("space")
    pn = Plan(support, kernel, v_ext, orb_count, space_count)
    n, C = pn.orbs, len(pn.chunks)
    vmem = pl.BlockSpec(memory_space=pltpu.VMEM)
    dma = pltpu.SemaphoreType.DMA
    density, packed = pl.pallas_call(
        functools.partial(body, pn),
        out_shape=(
            jax.ShapeDtypeStruct(v_ext.shape, F32),
            jax.ShapeDtypeStruct((pn.pairs, LANES), F32),
        ),
        in_specs=[vmem] * 7,
        out_specs=(vmem, vmem),
        scratch_shapes=[
            pltpu.VMEM((LANES, LANES), F32),
            pltpu.VMEM((pn.pairs, LANES), F32),
            pltpu.VMEM((pn.funcs, pn.total, LANES), BF16),
            pltpu.VMEM((n, pn.block, pn.width), BF16),
            pltpu.VMEM((pn.blocks, pn.block, pn.width), BF16),
            pltpu.VMEM((pn.blocks, pn.pairs, LANES), F32),
            pltpu.VMEM((pn.total, pn.width), BF16),
            pltpu.VMEM((pn.total, pn.total), F32),
            pltpu.VMEM((pn.total, pn.width), F32),
            pltpu.VMEM((pn.total, pn.total), F32),
            pltpu.VMEM((pn.total, pn.width), BF16),
            pltpu.VMEM((n, pn.rows, pn.points), F32),
            pltpu.VMEM((pn.blocks, pn.pairs, LANES), BF16),
            pltpu.VMEM((2 * pn.blocks, pn.pairs, LANES), BF16),
            dma((n, C)),
            dma((n, C)),
            dma((n, 2)),
            dma((n, 2)),
            dma((2 * n,)),
            dma((2 * n,)),
            dma((n,)),
            dma((n,)),
            dma((2 * pn.blocks,)),
            dma((2 * pn.blocks,)),
        ],
        compiler_params=pltpu.CompilerParams(collective_id=0, has_side_effects=True),
        name="grain",
    )(
        jnp.transpose(kernel, (1, 2, 0)),
        pair_owner.reshape(1, pn.pairs),
        pair_partner.reshape(1, pn.pairs),
        pair_live.reshape(1, pn.pairs),
        anchor.reshape(1, pn.atoms),
        jnp.transpose(support, (1, 2, 0, 3)),
        v_ext,
    )
    density, blocks = pl.pallas_call(
        functools.partial(finish, pn),
        out_shape=(
            jax.ShapeDtypeStruct(v_ext.shape, F32),
            jax.ShapeDtypeStruct((pn.funcs, pn.funcs, pn.pairs), F32),
        ),
        in_specs=[vmem] * 2,
        out_specs=(vmem, vmem),
        name="finish",
    )(density, packed)
    return (density, jnp.transpose(blocks, (2, 0, 1)))


def solution(mesh):
    placed = (
        P(("shift", "space", "orb"), None, None, "grid"),
        P(("shift", "space", "orb")),
        P(("shift", "space", "orb"), None, None),
        P(("shift", "space", "orb")),
        P(("shift", "space", "orb")),
        P(("shift", "space", "orb")),
        P(("shift", "space"), "grid"),
    )
    return jax.shard_map(
        on_device,
        mesh=mesh,
        in_specs=placed,
        out_specs=(P(("shift", "space"), "grid"), P(("shift", "space", "orb"), None, None)),
        check_vma=False,
    )
```
